512 devices in a mesh: ctx: 32 (over y, x), db: 16 (over z, core).
Axes of the slice: x: 4, y: 8, z: 8, core: 2. Of those that a mesh axis runs over, the one named last changes fastest.
Arguments:
- stream: bfloat16 [12288, 4096], P('ctx', 'db'), may hold values from -6 to 6
- history: bfloat16 [8, 12288, 4096], P(None, 'ctx', 'db'), may hold values from -6 to 6
- dwa_weights: float32 [9], replicated, may hold values from -0.5 to 1
- w_query: bfloat16 [4096, 4096], P('ctx', 'db'), may hold values from -0.09375 to 0.09375
- w_out: bfloat16 [4096, 4096], P('db', 'ctx'), may hold values from -0.1875 to 0.1875
- encoded_kv: bfloat16 [16, 24, 128, 2, 4096], P('db', None, 'ctx'), may hold values from -340 to 340
- neighbour_ids: int32 [384], replicated, may hold values from 0 to 383, each once
Outputs:
- block_out: bfloat16 [12288, 4096], P('ctx', 'db')
- dense: bfloat16 [12288, 4096], P('ctx', 'db')
The draws below stay inside these ranges and needn't reach their ends.
Inputs may be any that keep to these rules, and one draw needn't show every extreme that they name: `neighbour_ids`: each stored neighbour is named by exactly one slot.
All inputs are finite; a program needn't handle non-finite values.
Results may differ from the reference program's by a relative error of at most 0.014.
The reference program's roundings to bfloat16 on the way count: a program that leaves them out, or rounds other values in their place, can miss the bound.
Values may be sent and summed in bfloat16 or wider, within the bound.
No kernel may reach another device: no remote copies, remote signals or barrier semaphores. Data moves between devices by JAX's collectives and lax.ppermute only.
A program may use at most 64 MiB of HBM per device.

```python
import jax
import jax.numpy as jnp
from jax import lax

D = 4096
HDIM = 128
LAYERS = 8
SPAN = 64
NLEN = 128
NNB = 2
TOKENS = 12288
SPANS = 192
NSTORE = 384
GROUPS = 16
NBG = 24
N_DB = 16


def draw_encoded_kv(key, part):
    shape = (GROUPS, NBG, NLEN, 2, D)
    first_key = jax.random.fold_in(key, 0)
    base = jnp.clip(jax.random.normal(first_key, shape, jnp.float32), -6.0, 6.0)
    spread = jnp.ones((GROUPS, NBG, NLEN, 1, 1), jnp.float32)
    factor = jnp.concatenate([2.5 * spread, jnp.ones_like(spread)], axis=3)
    return (base * factor).astype(jnp.bfloat16)


def with_spikes(entries, own_key, source, target, shards_of, factor):
    def block_of(axis_at):
        return (jnp.arange(entries.shape[axis_at]) // (entries.shape[axis_at] // shards_of)).reshape((-1,) + (1,) * (entries.ndim - 1 - axis_at))

    one_side = jax.random.permutation(own_key, shards_of)[block_of(target)]
    other_side = (block_of(target) + shards_of // 2) % shards_of
    return jnp.where((block_of(source) == one_side) | (block_of(source) == other_side), factor * entries, entries)


def steps_of(key, extent, shards, smallest, high):
    level, own = 1.0, jax.random.fold_in(key, 6)
    for position, parts in shards:
        steps = jnp.exp(jax.random.uniform(jax.random.fold_in(own, position), (parts,), jnp.float32, smallest / len(shards), high / len(shards)))
        level = level * jnp.repeat(steps, extent[position] // parts).reshape([-1 if axis == position else 1 for axis in range(len(extent))])
    return level


def noise(key, extent, scale, limit, pieces=(), dtype=jnp.bfloat16):
    values = scale * jax.random.normal(key, extent, jnp.float32)
    if pieces:
        values = values * steps_of(key, extent, pieces, -0.22, 0.18)
    return jnp.clip(values, -limit, limit).astype(dtype)


def heavy_noise(stream_key, shape, deviation, reach, cuts, heavy, dtype=jnp.bfloat16):
    result = deviation * jax.random.normal(stream_key, shape, jnp.float32)
    if cuts:
        result = result * steps_of(stream_key, shape, cuts, -0.22, 0.18)
    return jnp.clip(with_spikes(result, jax.random.fold_in(stream_key, 3), *heavy), -reach, reach).astype(dtype)


def setup_inputs(seed: int = 0) -> dict:
    key_of = jax.random.split(jax.random.key(seed), 8)
    return {
        "stream": noise(key_of[0], (TOKENS, D), 1.0, 6.0, ((0, 32), (1, 16))),
        "history": noise(key_of[1], (LAYERS, TOKENS, D), 1.0, 6.0, ((1, 32), (2, 16))),
        "dwa_weights": jnp.clip(jax.random.uniform(key_of[2], (LAYERS + 1,), jnp.float32, -0.5, 1.0), -0.5, 1.0),
        "w_query": noise(key_of[3], (D, D), D ** -0.5, 0.09375, ((0, 32), (1, 16))),
        "w_out": heavy_noise(key_of[4], (D, D), D ** -0.5, 0.1875, ((0, 16), (1, 32)), (0, 1, 32, 2.75)),
        "encoded_kv": draw_encoded_kv(jax.random.fold_in(key_of[7], 71), 0),
        "neighbour_ids": jax.random.permutation(key_of[6], NSTORE).astype(jnp.int32),
    }


def attend_one(span_queries, key_rows, value_rows):
    head_count = D // HDIM
    query_heads = span_queries.astype(jnp.float32).reshape(SPAN, head_count, HDIM)
    key_heads = key_rows.astype(jnp.float32).reshape(NNB * NLEN, head_count, HDIM)
    value_heads = value_rows.astype(jnp.float32).reshape(NNB * NLEN, head_count, HDIM)
    scores = jnp.einsum("qhd,khd->hqk", query_heads, key_heads) * (HDIM ** -0.5)
    row_max = jnp.max(scores, axis=-1, keepdims=True)
    exponent = jnp.exp(scores - row_max)
    weights = (exponent / jnp.sum(exponent, axis=-1, keepdims=True)).astype(jnp.bfloat16)
    mixed = jnp.einsum("hqk,khd->qhd", weights.astype(jnp.float32), value_heads)
    return mixed.astype(jnp.bfloat16).reshape(SPAN, D)


def reference(stream, history, dwa_weights, w_query, w_out, encoded_kv, neighbour_ids):
    queries = jnp.dot(stream, w_query, preferred_element_type=jnp.float32).astype(jnp.bfloat16)
    lead_rows = SPAN - 1
    shifted = jnp.concatenate([queries[lead_rows:], jnp.zeros((lead_rows, D), jnp.bfloat16)], 0)
    shifted = shifted.reshape(SPANS, SPAN, D)
    store = encoded_kv.reshape(NSTORE, NLEN, 2, D)
    span_pairs = neighbour_ids.reshape(SPANS, NNB).astype(jnp.int32)

    def one_span(operands):
        span_queries, span_ids = operands
        rows_kv = jnp.take(store, span_ids, axis=0).reshape(NNB * NLEN, 2, D)
        return attend_one(span_queries, rows_kv[:, 0], rows_kv[:, 1])

    mixed = lax.map(one_span, (shifted, span_pairs)).reshape(TOKENS, D)
    attended = jnp.concatenate([jnp.zeros((lead_rows, D), jnp.bfloat16), mixed[:TOKENS - lead_rows]], 0)
    group_width = D // N_DB
    total = jnp.zeros((TOKENS, D), jnp.float32)
    for group in range(N_DB):
        partial_value = jnp.dot(attended[:, group * group_width:(group + 1) * group_width],
                          w_out[group * group_width:(group + 1) * group_width],
                          preferred_element_type=jnp.float32)
        rounded = lax.optimization_barrier(partial_value.astype(jnp.bfloat16))
        total = total + rounded.astype(jnp.float32)
    block = stream.astype(jnp.float32) + total
    dense = dwa_weights[LAYERS] * block
    for layer in range(LAYERS):
        dense = dense + dwa_weights[layer] * history[layer].astype(jnp.float32)
    return block.astype(jnp.bfloat16), dense.astype(jnp.bfloat16)
```

```python
import jax
import jax.numpy as jnp
from jax import lax
from jax.experimental import pallas as pl
from jax.experimental.pallas import tpu as pltpu
from jax.sharding import Mesh, PartitionSpec as P

ROOM = pltpu.CompilerParams(vmem_limit_bytes=24 * 1024 * 1024)
HDIM = 128
SPAN = 64
NNB = 2
LEAD = SPAN - 1
CTX = ("y", "x")
DB = ("z", "core")


def any_space():
    return pl.BlockSpec(memory_space=pl.ANY)


def vmem_space():
    return pl.BlockSpec(memory_space=pltpu.VMEM)


def split_heads_kernel(source, out, sems):
    heads, local_heads = source.shape[4] // HDIM, out.shape[2]
    copies = []
    for head in range(heads):
        target = out.at[head // local_heads, :, head % local_heads]
        copies.append(
            pltpu.make_async_copy(
                source.at[0, :, :, :, pl.ds(head * HDIM, HDIM)], target, sems.at[head]
            )
        )
        copies[-1].start()
    for copy in copies:
        copy.wait()


def split_heads(encoded, local_heads):
    _, held, rows, pair, width = encoded.shape
    heads = width // HDIM
    return pl.pallas_call(
        split_heads_kernel,
        out_shape=jax.ShapeDtypeStruct(
            (heads // local_heads, held, local_heads, rows, pair, HDIM), encoded.dtype
        ),
        in_specs=[any_space()],
        out_specs=vmem_space(),
        scratch_shapes=[pltpu.SemaphoreType.DMA((heads,))],
        compiler_params=ROOM,
        name="split_heads",
    )(encoded)


def pick_kernel(ids, store, out):
    def body(i, carry):
        out[i] = store[ids[i]]
        return carry

    lax.fori_loop(0, out.shape[0], body, 0, unroll=8)


def pick(ids, store):
    count = ids.shape[0]
    block = store.shape[1:]
    return pl.pallas_call(
        pick_kernel,
        out_shape=jax.ShapeDtypeStruct((count,) + block, store.dtype),
        grid_spec=pltpu.PrefetchScalarGridSpec(
            num_scalar_prefetch=1,
            grid=(1,),
            in_specs=[pl.BlockSpec(store.shape, lambda i, s: (0, 0, 0))],
            out_specs=pl.BlockSpec((count,) + block, lambda i, s: (0, 0, 0)),
        ),
        compiler_params=ROOM,
        name="pick",
    )(ids, store)


def attend_kernel(q_ref, kv_ref, o_ref):
    slabs, slots, heads, rows, _ = kv_ref.shape
    keys = slabs * NNB * rows
    lane = lax.broadcasted_iota(jnp.int32, (SPAN, keys), 1)
    is_key = (lane & 1) == 0
    for span in range(slots // NNB):
        tokens = slice(span * SPAN, (span + 1) * SPAN)
        for head in range(heads):
            columns = slice(head * HDIM, (head + 1) * HDIM)
            rows_kv = kv_ref[:, NNB * span : NNB * span + NNB, head].reshape(keys, HDIM)
            scores = lax.dot_general(
                q_ref[tokens, columns],
                rows_kv,
                (((1,), (1,)), ((), ())),
                preferred_element_type=jnp.float32,
            ) * HDIM ** (-0.5)
            scores = jnp.where(is_key, scores, -jnp.inf)
            row_max = jnp.max(scores, axis=-1, keepdims=True)
            exponent = jnp.exp(scores - row_max)
            weights = exponent / jnp.sum(exponent, axis=-1, keepdims=True)
            on_values = pltpu.roll(weights, 1, 1).astype(jnp.bfloat16)
            mixed = lax.dot_general(
                on_values, rows_kv, (((1,), (0,)), ((), ())), preferred_element_type=jnp.float32
            )
            o_ref[tokens, columns] = mixed.astype(jnp.bfloat16)


def attend(queries, kv):
    return pl.pallas_call(
        attend_kernel,
        out_shape=jax.ShapeDtypeStruct(queries.shape, jnp.bfloat16),
        in_specs=[vmem_space(), vmem_space()],
        out_specs=vmem_space(),
        compiler_params=ROOM,
        name="attend",
    )(queries, kv)


def shifted(block, distance):
    count = lax.axis_size(CTX)
    route = [(i - distance, i) for i in range(count) if 0 <= i - distance < count]
    return lax.ppermute(block, CTX, route)


def ring(count, step):
    return [(i, (i + step) % count) for i in range(count)]


def around(block, axis):
    count = lax.axis_size(axis)
    parts = {0: block}
    right = left = block
    for step in range(1, count // 2 + 1):
        right = lax.ppermute(right, axis, ring(count, 1))
        parts[-step] = right
        if step < count - count // 2:
            left = lax.ppermute(left, axis, ring(count, -1))
            parts[step] = left
    return jnp.stack([parts[i] for i in sorted(parts)])


def partner(block):
    return lax.ppermute(block, "core", [(0, 1), (1, 0)])


def project_kernel(place, mine, other, weights, out):
    steps, _, depth = mine.shape
    z, core = place[0], place[1]

    def body(i, total):
        at = lax.rem(z + i + steps - steps // 2, steps) * 2
        w_mine = weights[pl.ds((at + core) * 2, 2), 0].reshape(depth, -1)
        w_other = weights[pl.ds((at + 1 - core) * 2, 2), 0].reshape(depth, -1)
        total += jnp.dot(mine[i], w_mine, preferred_element_type=jnp.float32)
        total += jnp.dot(other[i], w_other, preferred_element_type=jnp.float32)
        return total

    total = lax.fori_loop(0, steps, body, jnp.zeros(out.shape, jnp.float32))
    out[...] = total.astype(out.dtype)


def project(place, mine, other, weights):
    rows, width = mine.shape[1], weights.shape[3]
    return pl.pallas_call(
        project_kernel,
        out_shape=jax.ShapeDtypeStruct((rows, width), jnp.bfloat16),
        in_specs=[pl.BlockSpec(memory_space=pltpu.SMEM)] + [vmem_space()] * 3,
        out_specs=vmem_space(),
        compiler_params=ROOM,
        name="project",
    )(place, mine, other, weights)


def finish_kernel(dwa, attended, weights, stream, past, block_out, dense_out):
    groups, _, depth = attended.shape

    def body(g, total):
        w = weights[pl.ds(g * 2, 2), 1].reshape(depth, -1)
        part = jnp.dot(attended[g], w, preferred_element_type=jnp.float32)
        return total + part.astype(jnp.bfloat16).astype(jnp.float32)

    total = lax.fori_loop(0, groups, body, jnp.zeros(stream.shape, jnp.float32))
    block = stream[...].astype(jnp.float32) + total
    block_out[...] = block.astype(block_out.dtype)
    dense_out[...] = (dwa[dwa.shape[0] - 1] * block + past[...]).astype(dense_out.dtype)


def finish(dwa, attended, weights, stream, past):
    shape = jax.ShapeDtypeStruct(stream.shape, jnp.bfloat16)
    return pl.pallas_call(
        finish_kernel,
        out_shape=(shape, shape),
        in_specs=[pl.BlockSpec(memory_space=pltpu.SMEM)] + [vmem_space()] * 4,
        out_specs=(vmem_space(), vmem_space()),
        compiler_params=ROOM,
        name="finish",
    )(dwa, attended, weights, stream, past)


def columns_here(w_out):
    ctx_count, db_count = lax.axis_size(CTX), lax.axis_size(DB)
    odd = lax.rem(lax.axis_index(CTX), 2)
    half = w_out.shape[0] // 2
    pieces = []
    for flip in range(2):
        route = [
            (c * db_count + d, (2 * d + (c + flip) % 2) * db_count + c // 2)
            for c in range(ctx_count)
            for d in range(db_count)
        ]
        row = (odd + flip) % 2 * half
        send = lax.dynamic_slice_in_dim(w_out, row, half, 0)
        pieces.append(lax.ppermute(send, CTX + DB, route))
    straight = jnp.concatenate(pieces, 1)
    crossed = jnp.concatenate(pieces[::-1], 1)
    return jnp.where(odd == 0, straight, crossed)


def on_device(stream, history, dwa_weights, w_query, w_out, encoded_kv, neighbour_ids):
    tok_rows = stream.shape[0]
    local_heads = w_query.shape[1] // HDIM
    ctx_count = lax.axis_size(CTX)
    db_count = lax.axis_size(DB)
    slots = neighbour_ids.shape[0] // ctx_count
    slab_rows = 2 * encoded_kv.shape[2]
    place = jnp.stack([lax.axis_index("z"), lax.axis_index("core")]).astype(jnp.int32)

    weights = lax.all_gather(jnp.stack([w_query, columns_here(w_out)]), CTX, axis=0)
    after = shifted(stream[:SPAN], -1)
    own_spans = jnp.concatenate([stream[LEAD:], after[:LEAD]], 0)
    past = jnp.sum(history.astype(jnp.float32) * dwa_weights[:-1, None, None], axis=0)

    by_head = split_heads(encoded_kv, local_heads)
    store = lax.all_to_all(
        by_head.reshape(db_count, -1, HDIM), DB, split_axis=0, concat_axis=0, tiled=True
    )
    picked = pick(neighbour_ids, store.reshape(-1, local_heads * slab_rows, HDIM))
    own_spans, picked = lax.optimization_barrier((own_spans, picked))
    arrived = lax.all_to_all(
        picked.reshape(ctx_count, -1, HDIM), CTX, split_axis=0, concat_axis=0, tiled=True
    ).reshape(ctx_count, slots, local_heads, slab_rows, HDIM)
    mine = around(own_spans, "z")
    queries = project(place, mine, partner(mine), weights)
    mixed = attend(queries, arrived)
    before = shifted(mixed[tok_rows - SPAN :], 1)
    attended = jnp.concatenate([before[1:], mixed[: tok_rows - LEAD]], 0)
    everyone = lax.all_gather(attended, DB, axis=0)
    return finish(dwa_weights, everyone, weights, stream, past)


def solution(mesh):
    devices = mesh.devices
    cores = 2
    z = devices.shape[1] // cores
    x = 4
    y = devices.shape[0] // x
    split = Mesh(devices.reshape(y, x, z, cores), ("y", "x", "z", "core"))
    placed = (
        P(CTX, DB),
        P(None, CTX, DB),
        P(),
        P(CTX, DB),
        P(DB, CTX),
        P(DB, None, CTX, None, None),
        P(),
    )
    return jax.shard_map(
        on_device,
        mesh=split,
        in_specs=placed,
        out_specs=(P(CTX, DB), P(CTX, DB)),
        check_vma=False,
    )
```

```python
import functools

import jax
import jax.numpy as jnp
from jax import lax
from jax.experimental import pallas as pl
from jax.experimental.pallas import tpu as pltpu
from jax.sharding import Mesh, PartitionSpec as P

ROOM = pltpu.CompilerParams(vmem_limit_bytes=24 * 1024 * 1024)
HDIM = 128
SPAN = 64
NNB = 2
LEAD = SPAN - 1
CTX = ("y", "x")
DB = ("z", "core")


def any_space():
    return pl.BlockSpec(memory_space=pl.ANY)


def vmem_space():
    return pl.BlockSpec(memory_space=pltpu.VMEM)


def split_heads_kernel(source, out, sems):
    heads, local_heads = source.shape[4] // HDIM, out.shape[2]
    copies = []
    for head in range(heads):
        target = out.at[head // local_heads, :, head % local_heads]
        copies.append(
            pltpu.make_async_copy(
                source.at[0, :, :, :, pl.ds(head * HDIM, HDIM)], target, sems.at[head]
            )
        )
        copies[-1].start()
    for copy in copies:
        copy.wait()


def split_heads(encoded, local_heads):
    _, held, rows, pair, width = encoded.shape
    heads = width // HDIM
    return pl.pallas_call(
        split_heads_kernel,
        out_shape=jax.ShapeDtypeStruct(
            (heads // local_heads, held, local_heads, rows, pair, HDIM), encoded.dtype
        ),
        in_specs=[any_space()],
        out_specs=vmem_space(),
        scratch_shapes=[pltpu.SemaphoreType.DMA((heads,))],
        compiler_params=ROOM,
        name="split_heads",
    )(encoded)


def pick_kernel(ids, store, out):
    def body(i, carry):
        out[i] = store[ids[i]]
        return carry

    lax.fori_loop(0, out.shape[0], body, 0, unroll=8)


def pick(ids, store):
    count = ids.shape[0]
    block = store.shape[1:]
    return pl.pallas_call(
        pick_kernel,
        out_shape=jax.ShapeDtypeStruct((count,) + block, store.dtype),
        grid_spec=pltpu.PrefetchScalarGridSpec(
            num_scalar_prefetch=1,
            grid=(1,),
            in_specs=[pl.BlockSpec(store.shape, lambda i, s: (0, 0, 0))],
            out_specs=pl.BlockSpec((count,) + block, lambda i, s: (0, 0, 0)),
        ),
        compiler_params=ROOM,
        name="pick",
    )(ids, store)


def attend_kernel(first, q_ref, kv_ref, o_ref):
    slabs, _, heads, rows, _ = kv_ref.shape
    keys = slabs * NNB * rows
    lane = lax.broadcasted_iota(jnp.int32, (SPAN, keys), 1)
    is_key = (lane & 1) == 0
    for at in range(o_ref.shape[0] // SPAN):
        span = first + at
        tokens = slice(span * SPAN, (span + 1) * SPAN)
        for head in range(heads):
            columns = slice(head * HDIM, (head + 1) * HDIM)
            rows_kv = kv_ref[:, NNB * span : NNB * span + NNB, head].reshape(keys, HDIM)
            scores = lax.dot_general(
                q_ref[tokens, columns],
                rows_kv,
                (((1,), (1,)), ((), ())),
                preferred_element_type=jnp.float32,
            ) * HDIM ** (-0.5)
            scores = jnp.where(is_key, scores, -jnp.inf)
            row_max = jnp.max(scores, axis=-1, keepdims=True)
            exponent = jnp.exp(scores - row_max)
            weights = exponent / jnp.sum(exponent, axis=-1, keepdims=True)
            on_values = pltpu.roll(weights, 1, 1).astype(jnp.bfloat16)
            mixed = lax.dot_general(
                on_values, rows_kv, (((1,), (0,)), ((), ())), preferred_element_type=jnp.float32
            )
            o_ref[at * SPAN : (at + 1) * SPAN, columns] = mixed.astype(jnp.bfloat16)


def attend(queries, kv, first, spans):
    return pl.pallas_call(
        functools.partial(attend_kernel, first),
        out_shape=jax.ShapeDtypeStruct((spans * SPAN, queries.shape[1]), jnp.bfloat16),
        in_specs=[vmem_space(), vmem_space()],
        out_specs=vmem_space(),
        compiler_params=ROOM,
    )(queries, kv)


def shifted(block, distance):
    count = lax.axis_size(CTX)
    route = [(i - distance, i) for i in range(count) if 0 <= i - distance < count]
    return lax.ppermute(block, CTX, route)


def ring(count, step):
    return [(i, (i + step) % count) for i in range(count)]


def around(block, axis):
    count = lax.axis_size(axis)
    parts = {0: block}
    right = left = block
    for step in range(1, count // 2 + 1):
        right = lax.ppermute(right, axis, ring(count, 1))
        parts[-step] = right
        if step < count - count // 2:
            left = lax.ppermute(left, axis, ring(count, -1))
            parts[step] = left
    return jnp.stack([parts[i] for i in sorted(parts)])


def partner(block):
    return lax.ppermute(block, "core", [(0, 1), (1, 0)])


def project_kernel(place, mine, other, weights, out):
    steps, _, depth = mine.shape
    z, core = place[0], place[1]

    def body(i, total):
        at = lax.rem(z + i + steps - steps // 2, steps) * 2
        w_mine = weights[pl.ds((at + core) * 2, 2)].reshape(depth, -1)
        w_other = weights[pl.ds((at + 1 - core) * 2, 2)].reshape(depth, -1)
        total += jnp.dot(mine[i], w_mine, preferred_element_type=jnp.float32)
        total += jnp.dot(other[i], w_other, preferred_element_type=jnp.float32)
        return total

    total = lax.fori_loop(0, steps, body, jnp.zeros(out.shape, jnp.float32))
    out[...] = total.astype(out.dtype)


def project(place, mine, other, weights):
    rows, width = mine.shape[1], weights.shape[2]
    return pl.pallas_call(
        project_kernel,
        out_shape=jax.ShapeDtypeStruct((rows, width), jnp.bfloat16),
        in_specs=[pl.BlockSpec(memory_space=pltpu.SMEM)] + [vmem_space()] * 3,
        out_specs=vmem_space(),
        compiler_params=ROOM,
        name="project",
    )(place, mine, other, weights)


def finish_kernel(x, dwa, attended, weights, stream, past, block_out, dense_out, total):
    step = pl.program_id(0)
    across, _, depth, _ = weights.shape

    @pl.when(step == 0)
    def _():
        total[...] = jnp.zeros(total.shape, jnp.float32)

    pieces = attended.shape[2] // depth
    for g in range(attended.shape[0]):
        part = jnp.zeros(total.shape, jnp.float32)
        for piece in range(pieces):
            at = lax.rem(g * pieces + piece + across - x[0], across)
            part += jnp.dot(
                attended[g, :, piece * depth : (piece + 1) * depth],
                weights[at, 0],
                preferred_element_type=jnp.float32,
            )
        total[...] += part.astype(jnp.bfloat16).astype(jnp.float32)

    @pl.when(step == pl.num_programs(0) - 1)
    def _():
        block = stream[...].astype(jnp.float32) + total[...]
        block_out[...] = block.astype(block_out.dtype)
        dense_out[...] = (dwa[dwa.shape[0] - 1] * block + past[...]).astype(dense_out.dtype)


def finish(x, dwa, attended, weights, stream, past):
    groups, rows, depth = attended.shape
    across, along, cut, width = weights.shape
    here = groups // along
    scalars = pl.BlockSpec(memory_space=pltpu.SMEM)
    whole = pl.BlockSpec(stream.shape, lambda i: (0, 0))
    shape = jax.ShapeDtypeStruct(stream.shape, jnp.bfloat16)
    return pl.pallas_call(
        finish_kernel,
        grid=(along,),
        out_shape=(shape, shape),
        in_specs=[
            scalars,
            scalars,
            pl.BlockSpec((here, rows, depth), lambda i: (i, 0, 0)),
            pl.BlockSpec((across, 1, cut, width), lambda i: (0, i, 0, 0)),
            whole,
            whole,
        ],
        out_specs=(whole, whole),
        scratch_shapes=[pltpu.VMEM(stream.shape, jnp.float32)],
        name="finish",
    )(x, dwa, attended, weights, stream, past)


def columns_here(w_out):
    ctx_count, db_count = lax.axis_size(CTX), lax.axis_size(DB)
    odd = lax.rem(lax.axis_index(CTX), 2)
    half = w_out.shape[0] // 2
    pieces = []
    for flip in range(2):
        route = [
            (c * db_count + d, (2 * d + (c + flip) % 2) * db_count + c // 2)
            for c in range(ctx_count)
            for d in range(db_count)
        ]
        row = (odd + flip) % 2 * half
        send = lax.dynamic_slice_in_dim(w_out, row, half, 0)
        pieces.append(lax.ppermute(send, CTX + DB, route))
    straight = jnp.concatenate(pieces, 1)
    crossed = jnp.concatenate(pieces[::-1], 1)
    return jnp.where(odd == 0, straight, crossed)


def along_x(block):
    count = lax.axis_size("x")
    half = block.shape[0] // 2
    before = lax.ppermute(block, "x", ring(count, 1))
    after = lax.ppermute(block, "x", ring(count, -1))
    low = lax.ppermute(before[:half], "x", ring(count, 1))
    high = lax.ppermute(after[half:], "x", ring(count, -1))
    return jnp.stack([block, after, jnp.concatenate([low, high], 0), before])


def on_device(stream, history, dwa_weights, w_query, w_out, encoded_kv, neighbour_ids):
    tok_rows, _ = stream.shape
    local_heads = w_query.shape[1] // HDIM
    ctx_count = lax.axis_size(CTX)
    db_count = lax.axis_size(DB)
    slots = neighbour_ids.shape[0] // ctx_count
    slab_rows = 2 * encoded_kv.shape[2]
    place = jnp.stack([lax.axis_index("z"), lax.axis_index("core")]).astype(jnp.int32)
    x = lax.axis_index("x").astype(jnp.int32).reshape(1)

    w_in = lax.all_gather(w_query, CTX, axis=0)
    by_head = split_heads(encoded_kv, local_heads)
    store = lax.all_to_all(
        by_head.reshape(db_count, -1, HDIM), DB, split_axis=0, concat_axis=0, tiled=True
    )
    after = shifted(stream[:SPAN], -1)
    own_spans = jnp.concatenate([stream[LEAD:], after[:LEAD]], 0)
    turned = columns_here(w_out)
    turned = lax.all_gather(turned, "y", axis=0)

    picked = pick(neighbour_ids, store.reshape(-1, local_heads * slab_rows, HDIM))
    own_spans, turned, picked = lax.optimization_barrier((own_spans, turned, picked))
    arrived = lax.all_to_all(
        picked.reshape(ctx_count, -1, HDIM), CTX, split_axis=0, concat_axis=0, tiled=True
    ).reshape(ctx_count, slots, local_heads, slab_rows, HDIM)
    mine = around(own_spans, "z")
    past = jnp.sum(history.astype(jnp.float32) * dwa_weights[:-1, None, None], axis=0)
    queries = project(place, mine, partner(mine), w_in)
    spans = tok_rows // SPAN
    last = attend(queries, arrived, spans - 1, 1)
    before = shifted(last, 1)
    rest = attend(queries, arrived, 0, spans - 1)
    attended = jnp.concatenate([before[1:], rest, last[:1]], 0)
    attended, turned = lax.optimization_barrier((attended, turned))
    everyone = lax.all_gather(attended, DB, axis=0)
    columns = along_x(turned)
    return finish(x, dwa_weights, everyone, columns, stream, past)


def solution(mesh):
    devices = mesh.devices
    cores = 2
    z = devices.shape[1] // cores
    x = 4
    y = devices.shape[0] // x
    split = Mesh(devices.reshape(y, x, z, cores), ("y", "x", "z", "core"))
    placed = (
        P(CTX, DB),
        P(None, CTX, DB),
        P(),
        P(CTX, DB),
        P(DB, CTX),
        P(DB, None, CTX, None, None),
        P(),
    )
    return jax.shard_map(
        on_device,
        mesh=split,
        in_specs=placed,
        out_specs=(P(CTX, DB), P(CTX, DB)),
        check_vma=False,
    )
```

```python
import functools

import jax
import jax.numpy as jnp
from jax import lax
from jax.experimental import pallas as pl
from jax.experimental.pallas import tpu as pltpu
from jax.sharding import Mesh, PartitionSpec as P

ROOM = pltpu.CompilerParams(vmem_limit_bytes=24 * 1024 * 1024)
HDIM = 128
SPAN = 64
NNB = 2
LEAD = SPAN - 1
CTX = ("y", "x")
DB = ("z", "core")


def any_space():
    return pl.BlockSpec(memory_space=pl.ANY)


def vmem_space():
    return pl.BlockSpec(memory_space=pltpu.VMEM)


def split_heads_kernel(source, out, sems):
    heads, local_heads = source.shape[4] // HDIM, out.shape[2]
    copies = []
    for head in range(heads):
        target = out.at[head // local_heads, :, head % local_heads]
        copies.append(
            pltpu.make_async_copy(
                source.at[0, :, :, :, pl.ds(head * HDIM, HDIM)], target, sems.at[head]
            )
        )
        copies[-1].start()
    for copy in copies:
        copy.wait()


def split_heads(encoded, local_heads):
    _, held, rows, pair, width = encoded.shape
    heads = width // HDIM
    return pl.pallas_call(
        split_heads_kernel,
        out_shape=jax.ShapeDtypeStruct(
            (heads // local_heads, held, local_heads, rows, pair, HDIM), encoded.dtype
        ),
        in_specs=[any_space()],
        out_specs=vmem_space(),
        scratch_shapes=[pltpu.SemaphoreType.DMA((heads,))],
        compiler_params=ROOM,
        name="split_heads",
    )(encoded)


def pick_kernel(ids, store, out):
    def body(i, carry):
        out[i] = store[ids[i]]
        return carry

    lax.fori_loop(0, out.shape[0], body, 0, unroll=8)


def pick(ids, store):
    count = ids.shape[0]
    block = store.shape[1:]
    return pl.pallas_call(
        pick_kernel,
        out_shape=jax.ShapeDtypeStruct((count,) + block, store.dtype),
        grid_spec=pltpu.PrefetchScalarGridSpec(
            num_scalar_prefetch=1,
            grid=(1,),
            in_specs=[pl.BlockSpec(store.shape, lambda i, s: (0, 0, 0))],
            out_specs=pl.BlockSpec((count,) + block, lambda i, s: (0, 0, 0)),
        ),
        compiler_params=ROOM,
        name="pick",
    )(ids, store)


def attend_kernel(first, q_ref, kv_ref, o_ref):
    slabs, _, heads, rows, _ = kv_ref.shape
    keys = slabs * NNB * rows
    lane = lax.broadcasted_iota(jnp.int32, (SPAN, keys), 1)
    is_key = (lane & 1) == 0
    for at in range(o_ref.shape[0] // SPAN):
        span = first + at
        tokens = slice(span * SPAN, (span + 1) * SPAN)
        for head in range(heads):
            columns = slice(head * HDIM, (head + 1) * HDIM)
            rows_kv = kv_ref[:, NNB * span : NNB * span + NNB, head].reshape(keys, HDIM)
            scores = lax.dot_general(
                q_ref[tokens, columns],
                rows_kv,
                (((1,), (1,)), ((), ())),
                preferred_element_type=jnp.float32,
            ) * HDIM ** (-0.5)
            scores = jnp.where(is_key, scores, -jnp.inf)
            row_max = jnp.max(scores, axis=-1, keepdims=True)
            exponent = jnp.exp(scores - row_max)
            weights = exponent / jnp.sum(exponent, axis=-1, keepdims=True)
            on_values = pltpu.roll(weights, 1, 1).astype(jnp.bfloat16)
            mixed = lax.dot_general(
                on_values, rows_kv, (((1,), (0,)), ((), ())), preferred_element_type=jnp.float32
            )
            o_ref[at * SPAN : (at + 1) * SPAN, columns] = mixed.astype(jnp.bfloat16)


def attend(queries, kv, first, spans):
    return pl.pallas_call(
        functools.partial(attend_kernel, first),
        out_shape=jax.ShapeDtypeStruct((spans * SPAN, queries.shape[1]), jnp.bfloat16),
        in_specs=[vmem_space(), vmem_space()],
        out_specs=vmem_space(),
        compiler_params=ROOM,
    )(queries, kv)


def shifted(block, distance):
    count = lax.axis_size(CTX)
    route = [(i - distance, i) for i in range(count) if 0 <= i - distance < count]
    return lax.ppermute(block, CTX, route)


def ring(count, step):
    return [(i, (i + step) % count) for i in range(count)]


STEPS = 4
BAND = 128


def project_kernel(x, blocks, weights, out, total):
    step = pl.program_id(0)
    across, _, depth, _ = weights.shape
    pieces = blocks.shape[2] // depth

    @pl.when(step == 0)
    def _():
        total[...] = jnp.zeros(total.shape, jnp.float32)

    for row in range(0, total.shape[0], BAND):
        rows = slice(row, row + BAND)
        value = total[rows, :]
        for g in range(blocks.shape[0]):
            for piece in range(pieces):
                column = g * pieces + piece
                at = lax.rem(column % across + across - x[0], across)
                value += jnp.dot(
                    blocks[g, rows, piece * depth : (piece + 1) * depth],
                    weights[at, column // across],
                    preferred_element_type=jnp.float32,
                )
        total[rows, :] = value

    @pl.when(step == pl.num_programs(0) - 1)
    def _():
        out[...] = total[...].astype(out.dtype)


def project(x, blocks, weights):
    groups, rows, depth = blocks.shape
    across, along, cut, width = weights.shape
    return pl.pallas_call(
        project_kernel,
        grid=(STEPS,),
        out_shape=jax.ShapeDtypeStruct((rows, width), jnp.bfloat16),
        in_specs=[
            pl.BlockSpec(memory_space=pltpu.SMEM),
            pl.BlockSpec((groups // STEPS, rows, depth), lambda i: (i, 0, 0)),
            pl.BlockSpec((across, along // STEPS, cut, width), lambda i: (0, i, 0, 0)),
        ],
        out_specs=pl.BlockSpec((rows, width), lambda i: (0, 0)),
        scratch_shapes=[pltpu.VMEM((rows, width), jnp.float32)],
        name="project",
    )(x, blocks, weights)


def finish_kernel(y, dwa, first, second, weights, stream, past, block_out, dense_out, total):
    step = pl.program_id(0)
    width = weights.shape[3]

    @pl.when(step == 0)
    def _():
        total[...] = jnp.zeros(total.shape, jnp.float32)

    for row in range(0, total.shape[0], BAND):
        rows = slice(row, row + BAND)
        value = total[rows, :]
        for which, blocks in enumerate((first, second)):
            groups, _, depth = blocks.shape
            matching = weights[which].reshape(groups, depth, width)
            for g in range(groups):
                part = jnp.dot(blocks[g, rows, :], matching[g], preferred_element_type=jnp.float32)
                value += part.astype(jnp.bfloat16).astype(jnp.float32)
        total[rows, :] = value

    @pl.when(step == pl.num_programs(0) - 1)
    def _():
        block = stream[...].astype(jnp.float32) + total[...]
        block_out[...] = block.astype(block_out.dtype)
        dense_out[...] = (dwa[dwa.shape[0] - 1] * block + past[...]).astype(dense_out.dtype)


def finish(y, dwa, blocks, weights, stream, past):
    groups, rows, depth = blocks.shape
    along, across, cut, width = weights.shape
    steps = along // 2
    here = groups // along

    def at(which):
        return lambda i, y: (lax.rem(y[0] + 2 * i + which + along - along // 2, along), 0, 0)

    whole = pl.BlockSpec((rows, width), lambda i, y: (0, 0))
    shape = jax.ShapeDtypeStruct(stream.shape, jnp.bfloat16)
    return pl.pallas_call(
        finish_kernel,
        out_shape=(shape, shape),
        grid_spec=pltpu.PrefetchScalarGridSpec(
            num_scalar_prefetch=1,
            grid=(steps,),
            in_specs=[
                pl.BlockSpec(memory_space=pltpu.SMEM),
                pl.BlockSpec((here, rows, depth), at(0)),
                pl.BlockSpec((here, rows, depth), at(1)),
                pl.BlockSpec((2, across, cut, width), lambda i, y: (i, 0, 0, 0)),
                whole,
                whole,
            ],
            out_specs=(whole, whole),
            scratch_shapes=[pltpu.VMEM(stream.shape, jnp.float32)],
        ),
        name="finish",
    )(y, dwa, blocks, blocks, weights, stream, past)


def around(block, axis):
    count = lax.axis_size(axis)
    parts = {0: block}
    right = left = block
    for step in range(1, count // 2 + 1):
        right = lax.ppermute(right, axis, ring(count, 1))
        parts[-step] = right
        if step < count - count // 2:
            left = lax.ppermute(left, axis, ring(count, -1))
            parts[step] = left
    return jnp.stack([parts[i] for i in sorted(parts)])


def columns_here(w_out):
    ctx_count, db_count = lax.axis_size(CTX), lax.axis_size(DB)
    odd = lax.rem(lax.axis_index(CTX), 2)
    half = w_out.shape[0] // 2
    pieces = []
    for flip in range(2):
        route = [
            (c * db_count + d, (2 * d + (c + flip) % 2) * db_count + c // 2)
            for c in range(ctx_count)
            for d in range(db_count)
        ]
        row = (odd + flip) % 2 * half
        send = lax.dynamic_slice_in_dim(w_out, row, half, 0)
        pieces.append(lax.ppermute(send, CTX + DB, route))
    straight = jnp.concatenate(pieces, 1)
    crossed = jnp.concatenate(pieces[::-1], 1)
    return jnp.where(odd == 0, straight, crossed)


def along_x(block):
    count = lax.axis_size("x")
    half = block.shape[0] // 2
    before = lax.ppermute(block, "x", ring(count, 1))
    after = lax.ppermute(block, "x", ring(count, -1))
    low = lax.ppermute(before[:half], "x", ring(count, 1))
    high = lax.ppermute(after[half:], "x", ring(count, -1))
    return jnp.stack([block, after, jnp.concatenate([low, high], 0), before])


def on_device(stream, history, dwa_weights, w_query, w_out, encoded_kv, neighbour_ids):
    tok_rows = stream.shape[0]
    local_heads = w_query.shape[1] // HDIM
    ctx_count = lax.axis_size(CTX)
    db_count = lax.axis_size(DB)
    slots = neighbour_ids.shape[0] // ctx_count
    slab_rows = 2 * encoded_kv.shape[2]
    x = lax.axis_index("x").astype(jnp.int32).reshape(1)
    y = lax.axis_index("y").astype(jnp.int32).reshape(1)

    after = shifted(stream[:SPAN], -1)
    own_spans = jnp.concatenate([stream[LEAD:], after[:LEAD]], 0)
    by_head = split_heads(encoded_kv, local_heads)
    store = lax.all_to_all(
        by_head.reshape(db_count, -1, HDIM), DB, split_axis=0, concat_axis=0, tiled=True
    )
    turned = columns_here(w_out)
    w_in = lax.all_gather(w_query, "y", axis=0)
    w_in = along_x(w_in)
    own_spans, store, turned = lax.optimization_barrier((own_spans, store, turned))
    features = lax.all_gather(own_spans, DB, axis=0)
    picked = pick(neighbour_ids, store.reshape(-1, local_heads * slab_rows, HDIM))
    arrived = lax.all_to_all(
        picked.reshape(ctx_count, -1, HDIM), CTX, split_axis=0, concat_axis=0, tiled=True
    ).reshape(ctx_count, slots, local_heads, slab_rows, HDIM)
    w_in, turned = lax.optimization_barrier((w_in, turned))
    turned = lax.all_gather(turned, "x", axis=0)
    past = jnp.sum(history.astype(jnp.float32) * dwa_weights[:-1, None, None], axis=0)
    queries = project(x, features, w_in)
    spans = tok_rows // SPAN
    last = attend(queries, arrived, spans - 1, 1)
    before = shifted(last, 1)
    rest = attend(queries, arrived, 0, spans - 1)
    attended = jnp.concatenate([before[1:], rest, last[:1]], 0)
    attended, turned = lax.optimization_barrier((attended, turned))
    everyone = lax.all_gather(attended, DB, axis=0)
    columns = around(turned, "y")
    return finish(y, dwa_weights, everyone, columns, stream, past)


def solution(mesh):
    devices = mesh.devices
    cores = 2
    z = devices.shape[1] // cores
    x = 4
    y = devices.shape[0] // x
    split = Mesh(devices.reshape(y, x, z, cores), ("y", "x", "z", "core"))
    placed = (
        P(CTX, DB),
        P(None, CTX, DB),
        P(),
        P(CTX, DB),
        P(DB, CTX),
        P(DB, None, CTX, None, None),
        P(),
    )
    return jax.shard_map(
        on_device,
        mesh=split,
        in_specs=placed,
        out_specs=(P(CTX, DB), P(CTX, DB)),
        check_vma=False,
    )
```

```python
import functools

import jax
import jax.numpy as jnp
from jax import lax
from jax.experimental import pallas as pl
from jax.experimental.pallas import tpu as pltpu
from jax.sharding import Mesh, PartitionSpec as P

ROOM = pltpu.CompilerParams(vmem_limit_bytes=24 * 1024 * 1024)
HDIM = 128
SPAN = 64
NNB = 2
LEAD = SPAN - 1
CTX = ("y", "x")
DB = ("z", "core")


def any_space():
    return pl.BlockSpec(memory_space=pl.ANY)


def vmem_space():
    return pl.BlockSpec(memory_space=pltpu.VMEM)


def split_heads_kernel(source, out, sems):
    heads, local_heads = source.shape[4] // HDIM, out.shape[2]
    copies = []
    for head in range(heads):
        target = out.at[head // local_heads, :, head % local_heads]
        copies.append(
            pltpu.make_async_copy(
                source.at[0, :, :, :, pl.ds(head * HDIM, HDIM)], target, sems.at[head]
            )
        )
        copies[-1].start()
    for copy in copies:
        copy.wait()


def split_heads(encoded, local_heads):
    _, held, rows, pair, width = encoded.shape
    heads = width // HDIM
    return pl.pallas_call(
        split_heads_kernel,
        out_shape=jax.ShapeDtypeStruct(
            (heads // local_heads, held, local_heads, rows, pair, HDIM), encoded.dtype
        ),
        in_specs=[any_space()],
        out_specs=vmem_space(),
        scratch_shapes=[pltpu.SemaphoreType.DMA((heads,))],
        name="split_heads",
    )(encoded)


def pick_kernel(ids, store, out):
    def body(i, carry):
        out[i] = store[ids[i]]
        return carry

    lax.fori_loop(0, out.shape[0], body, 0, unroll=8)


def pick(ids, store):
    count = ids.shape[0]
    block = store.shape[1:]
    return pl.pallas_call(
        pick_kernel,
        out_shape=jax.ShapeDtypeStruct((count,) + block, store.dtype),
        grid_spec=pltpu.PrefetchScalarGridSpec(
            num_scalar_prefetch=1,
            grid=(1,),
            in_specs=[pl.BlockSpec(store.shape, lambda i, s: (0, 0, 0))],
            out_specs=pl.BlockSpec((count,) + block, lambda i, s: (0, 0, 0)),
        ),
        compiler_params=ROOM,
        name="pick",
    )(ids, store)


def attend_kernel(first, q_ref, kv_ref, o_ref):
    slabs, _, heads, rows, _ = kv_ref.shape
    keys = slabs * NNB * rows
    lane = lax.broadcasted_iota(jnp.int32, (SPAN, keys), 1)
    is_key = (lane & 1) == 0
    for at in range(o_ref.shape[0] // SPAN):
        span = first + at
        tokens = slice(span * SPAN, (span + 1) * SPAN)
        for head in range(heads):
            columns = slice(head * HDIM, (head + 1) * HDIM)
            rows_kv = kv_ref[:, NNB * span : NNB * span + NNB, head].reshape(keys, HDIM)
            scores = lax.dot_general(
                q_ref[tokens, columns],
                rows_kv,
                (((1,), (1,)), ((), ())),
                preferred_element_type=jnp.float32,
            ) * HDIM ** (-0.5)
            scores = jnp.where(is_key, scores, -jnp.inf)
            row_max = jnp.max(scores, axis=-1, keepdims=True)
            exponent = jnp.exp(scores - row_max)
            weights = exponent / jnp.sum(exponent, axis=-1, keepdims=True)
            on_values = pltpu.roll(weights, 1, 1).astype(jnp.bfloat16)
            mixed = lax.dot_general(
                on_values, rows_kv, (((1,), (0,)), ((), ())), preferred_element_type=jnp.float32
            )
            o_ref[at * SPAN : (at + 1) * SPAN, columns] = mixed.astype(jnp.bfloat16)


def attend(queries, kv, first, spans):
    return pl.pallas_call(
        functools.partial(attend_kernel, first),
        out_shape=jax.ShapeDtypeStruct((spans * SPAN, queries.shape[1]), jnp.bfloat16),
        in_specs=[vmem_space(), vmem_space()],
        out_specs=vmem_space(),
        compiler_params=ROOM,
    )(queries, kv)


def shifted(block, distance):
    count = lax.axis_size(CTX)
    route = [(i - distance, i) for i in range(count) if 0 <= i - distance < count]
    return lax.ppermute(block, CTX, route)


def ring(count, step):
    return [(i, (i + step) % count) for i in range(count)]


STEPS = 4
BAND = 128


def project_kernel(blocks, weights, out, total):
    step = pl.program_id(0)

    @pl.when(step == 0)
    def _():
        total[...] = jnp.zeros(total.shape, jnp.float32)

    for row in range(0, total.shape[0], BAND):
        rows = slice(row, row + BAND)
        value = total[rows, :]
        for g in range(blocks.shape[0]):
            value += jnp.dot(blocks[g, rows, :], weights[g], preferred_element_type=jnp.float32)
        total[rows, :] = value

    @pl.when(step == pl.num_programs(0) - 1)
    def _():
        out[...] = total[...].astype(out.dtype)


def project(blocks, weights):
    groups, rows, depth = blocks.shape
    width = weights.shape[2]
    return pl.pallas_call(
        project_kernel,
        grid=(STEPS,),
        out_shape=jax.ShapeDtypeStruct((rows, width), jnp.bfloat16),
        in_specs=[
            pl.BlockSpec((groups // STEPS, rows, depth), lambda i: (i, 0, 0)),
            pl.BlockSpec((groups // STEPS, depth, width), lambda i: (i, 0, 0)),
        ],
        out_specs=pl.BlockSpec((rows, width), lambda i: (0, 0)),
        scratch_shapes=[pltpu.VMEM((rows, width), jnp.float32)],
        name="project",
    )(blocks, weights)


def finish_kernel(y, dwa, first, second, weights, stream, past, block_out, dense_out, total):
    step = pl.program_id(0)
    width = weights.shape[3]

    @pl.when(step == 0)
    def _():
        total[...] = jnp.zeros(total.shape, jnp.float32)

    for row in range(0, total.shape[0], BAND):
        rows = slice(row, row + BAND)
        value = total[rows, :]
        for which, blocks in enumerate((first, second)):
            groups, _, depth = blocks.shape
            matching = weights[which].reshape(groups, depth, width)
            for g in range(groups):
                part = jnp.dot(blocks[g, rows, :], matching[g], preferred_element_type=jnp.float32)
                value += part.astype(jnp.bfloat16).astype(jnp.float32)
        total[rows, :] = value

    @pl.when(step == pl.num_programs(0) - 1)
    def _():
        block = stream[...].astype(jnp.float32) + total[...]
        block_out[...] = block.astype(block_out.dtype)
        dense_out[...] = (dwa[dwa.shape[0] - 1] * block + past[...]).astype(dense_out.dtype)


def finish(y, dwa, blocks, weights, stream, past):
    groups, rows, depth = blocks.shape
    along, across, cut, width = weights.shape
    steps = along // 2
    here = groups // along

    def at(which):
        return lambda i, y: (lax.rem(y[0] + 2 * i + which + along - along // 2, along), 0, 0)

    whole = pl.BlockSpec((rows, width), lambda i, y: (0, 0))
    shape = jax.ShapeDtypeStruct(stream.shape, jnp.bfloat16)
    return pl.pallas_call(
        finish_kernel,
        out_shape=(shape, shape),
        grid_spec=pltpu.PrefetchScalarGridSpec(
            num_scalar_prefetch=1,
            grid=(steps,),
            in_specs=[
                pl.BlockSpec(memory_space=pltpu.SMEM),
                pl.BlockSpec((here, rows, depth), at(0)),
                pl.BlockSpec((here, rows, depth), at(1)),
                pl.BlockSpec((2, across, cut, width), lambda i, y: (i, 0, 0, 0)),
                whole,
                whole,
            ],
            out_specs=(whole, whole),
            scratch_shapes=[pltpu.VMEM(stream.shape, jnp.float32)],
        ),
        name="finish",
    )(y, dwa, blocks, blocks, weights, stream, past)


def around(block, axis):
    count = lax.axis_size(axis)
    parts = {0: block}
    right = left = block
    for step in range(1, count // 2 + 1):
        right = lax.ppermute(right, axis, ring(count, 1))
        parts[-step] = right
        if step < count - count // 2:
            left = lax.ppermute(left, axis, ring(count, -1))
            parts[step] = left
    return jnp.stack([parts[i] for i in sorted(parts)])


def columns_here(w_out):
    ctx_count, db_count = lax.axis_size(CTX), lax.axis_size(DB)
    odd = lax.rem(lax.axis_index(CTX), 2)
    half = w_out.shape[0] // 2
    pieces = []
    for flip in range(2):
        route = [
            (c * db_count + d, (2 * d + (c + flip) % 2) * db_count + c // 2)
            for c in range(ctx_count)
            for d in range(db_count)
        ]
        row = (odd + flip) % 2 * half
        send = lax.dynamic_slice_in_dim(w_out, row, half, 0)
        pieces.append(lax.ppermute(send, CTX + DB, route))
    straight = jnp.concatenate(pieces, 1)
    crossed = jnp.concatenate(pieces[::-1], 1)
    return jnp.where(odd == 0, straight, crossed)


def on_device(stream, history, dwa_weights, w_query, w_out, encoded_kv, neighbour_ids):
    tok_rows = stream.shape[0]
    local_heads = w_query.shape[1] // HDIM
    ctx_count = lax.axis_size(CTX)
    db_count = lax.axis_size(DB)
    slots = neighbour_ids.shape[0] // ctx_count
    slab_rows = 2 * encoded_kv.shape[2]
    y = lax.axis_index("y").astype(jnp.int32).reshape(1)
    width = stream.shape[1]

    features = lax.all_gather(stream, DB, axis=0)
    by_head = split_heads(encoded_kv, local_heads)
    store = lax.all_to_all(
        by_head.reshape(db_count, -1, HDIM), DB, split_axis=0, concat_axis=0, tiled=True
    )
    w_in = lax.all_gather(w_query, "x", axis=0)
    w_in = lax.all_gather(w_in, "y", axis=0)
    turned = columns_here(w_out)
    picked = pick(neighbour_ids, store.reshape(-1, local_heads * slab_rows, HDIM))
    turned, picked = lax.optimization_barrier((turned, picked))
    arrived = lax.all_to_all(
        picked.reshape(ctx_count, -1, HDIM), CTX, split_axis=0, concat_axis=0, tiled=True
    ).reshape(ctx_count, slots, local_heads, slab_rows, HDIM)
    turned = lax.all_gather(turned, "x", axis=0)
    w_in, turned = lax.optimization_barrier((w_in, turned))
    past = jnp.sum(history.astype(jnp.float32) * dwa_weights[:-1, None, None], axis=0)
    queries = project(features, w_in.reshape(db_count, width, -1))
    after = shifted(queries[:SPAN], -1)
    queries = jnp.concatenate([queries[LEAD:], after[:LEAD]], 0)
    spans = tok_rows // SPAN
    last = attend(queries, arrived, spans - 1, 1)
    before = shifted(last, 1)
    rest = attend(queries, arrived, 0, spans - 1)
    attended = jnp.concatenate([before[1:], rest, last[:1]], 0)
    attended, turned = lax.optimization_barrier((attended, turned))
    everyone = lax.all_gather(attended, DB, axis=0)
    columns = around(turned, "y")
    return finish(y, dwa_weights, everyone, columns, stream, past)


def solution(mesh):
    devices = mesh.devices
    cores = 2
    z = devices.shape[1] // cores
    x = 4
    y = devices.shape[0] // x
    split = Mesh(devices.reshape(y, x, z, cores), ("y", "x", "z", "core"))
    placed = (
        P(CTX, DB),
        P(None, CTX, DB),
        P(),
        P(CTX, DB),
        P(DB, CTX),
        P(DB, None, CTX, None, None),
        P(),
    )
    return jax.shard_map(
        on_device,
        mesh=split,
        in_specs=placed,
        out_specs=(P(CTX, DB), P(CTX, DB)),
        check_vma=False,
    )
```

```python
import functools

import jax
import jax.numpy as jnp
from jax import lax
from jax.experimental import pallas as pl
from jax.experimental.pallas import tpu as pltpu
from jax.sharding import Mesh, PartitionSpec as P

ROOM = pltpu.CompilerParams(vmem_limit_bytes=24 * 1024 * 1024)
HDIM = 128
SPAN = 64
NNB = 2
LEAD = SPAN - 1
CTX = ("y", "x")
DB = ("z", "core")


def any_space():
    return pl.BlockSpec(memory_space=pl.ANY)


def vmem_space():
    return pl.BlockSpec(memory_space=pltpu.VMEM)


def split_heads_kernel(source, out, sems):
    heads, local_heads = source.shape[4] // HDIM, out.shape[2]
    copies = []
    for head in range(heads):
        target = out.at[head // local_heads, :, head % local_heads]
        copies.append(
            pltpu.make_async_copy(
                source.at[0, :, :, :, pl.ds(head * HDIM, HDIM)], target, sems.at[head]
            )
        )
        copies[-1].start()
    for copy in copies:
        copy.wait()


def split_heads(encoded, local_heads):
    _, held, rows, pair, width = encoded.shape
    heads = width // HDIM
    return pl.pallas_call(
        split_heads_kernel,
        out_shape=jax.ShapeDtypeStruct(
            (heads // local_heads, held, local_heads, rows, pair, HDIM), encoded.dtype
        ),
        in_specs=[any_space()],
        out_specs=vmem_space(),
        scratch_shapes=[pltpu.SemaphoreType.DMA((heads,))],
        name="split_heads",
    )(encoded)


def pick_kernel(ids, store, out):
    def body(i, carry):
        out[i] = store[ids[i]]
        return carry

    lax.fori_loop(0, out.shape[0], body, 0, unroll=8)


def pick(ids, store):
    count = ids.shape[0]
    block = store.shape[1:]
    return pl.pallas_call(
        pick_kernel,
        out_shape=jax.ShapeDtypeStruct((count,) + block, store.dtype),
        grid_spec=pltpu.PrefetchScalarGridSpec(
            num_scalar_prefetch=1,
            grid=(1,),
            in_specs=[pl.BlockSpec(store.shape, lambda i, s: (0, 0, 0))],
            out_specs=pl.BlockSpec((count,) + block, lambda i, s: (0, 0, 0)),
        ),
        compiler_params=ROOM,
        name="pick",
    )(ids, store)


def attend_kernel(first, q_ref, kv_ref, o_ref):
    slabs, _, heads, rows, _ = kv_ref.shape
    keys = slabs * NNB * rows
    lane = lax.broadcasted_iota(jnp.int32, (SPAN, keys), 1)
    is_key = (lane & 1) == 0
    for at in range(o_ref.shape[0] // SPAN):
        span = first + at
        tokens = slice(span * SPAN, (span + 1) * SPAN)
        for head in range(heads):
            columns = slice(head * HDIM, (head + 1) * HDIM)
            rows_kv = kv_ref[:, NNB * span : NNB * span + NNB, head].reshape(keys, HDIM)
            scores = lax.dot_general(
                q_ref[tokens, columns],
                rows_kv,
                (((1,), (1,)), ((), ())),
                preferred_element_type=jnp.float32,
            ) * HDIM ** (-0.5)
            scores = jnp.where(is_key, scores, -jnp.inf)
            row_max = jnp.max(scores, axis=-1, keepdims=True)
            exponent = jnp.exp(scores - row_max)
            weights = exponent / jnp.sum(exponent, axis=-1, keepdims=True)
            on_values = pltpu.roll(weights, 1, 1).astype(jnp.bfloat16)
            mixed = lax.dot_general(
                on_values, rows_kv, (((1,), (0,)), ((), ())), preferred_element_type=jnp.float32
            )
            o_ref[at * SPAN : (at + 1) * SPAN, columns] = mixed.astype(jnp.bfloat16)


def attend(queries, kv, first, spans):
    return pl.pallas_call(
        functools.partial(attend_kernel, first),
        out_shape=jax.ShapeDtypeStruct((spans * SPAN, queries.shape[1]), jnp.bfloat16),
        in_specs=[vmem_space(), vmem_space()],
        out_specs=vmem_space(),
        compiler_params=ROOM,
    )(queries, kv)


def shifted(block, distance):
    count = lax.axis_size(CTX)
    route = [(i - distance, i) for i in range(count) if 0 <= i - distance < count]
    return lax.ppermute(block, CTX, route)


def ring(count, step):
    return [(i, (i + step) % count) for i in range(count)]


def around(block, axis):
    count = lax.axis_size(axis)
    parts = {0: block}
    right = left = block
    for step in range(1, count // 2 + 1):
        right = lax.ppermute(right, axis, ring(count, 1))
        parts[-step] = right
        if step < count - count // 2:
            left = lax.ppermute(left, axis, ring(count, -1))
            parts[step] = left
    return jnp.stack([parts[i] for i in sorted(parts)])


def partner(block):
    return lax.ppermute(block, "core", [(0, 1), (1, 0)])


def project_kernel(place, mine, other, weights, out):
    steps, _, depth = mine.shape
    z, core = place[0], place[1]

    def body(i, total):
        at = lax.rem(z + i + steps - steps // 2, steps) * 2
        w_mine = weights[pl.ds((at + core) * 2, 2)].reshape(depth, -1)
        w_other = weights[pl.ds((at + 1 - core) * 2, 2)].reshape(depth, -1)
        total += jnp.dot(mine[i], w_mine, preferred_element_type=jnp.float32)
        total += jnp.dot(other[i], w_other, preferred_element_type=jnp.float32)
        return total

    total = lax.fori_loop(0, steps, body, jnp.zeros(out.shape, jnp.float32))
    out[...] = total.astype(out.dtype)


def project(place, mine, other, weights):
    rows, width = mine.shape[1], weights.shape[2]
    return pl.pallas_call(
        project_kernel,
        out_shape=jax.ShapeDtypeStruct((rows, width), jnp.bfloat16),
        in_specs=[pl.BlockSpec(memory_space=pltpu.SMEM)] + [vmem_space()] * 3,
        out_specs=vmem_space(),
        compiler_params=ROOM,
        name="project",
    )(place, mine, other, weights)


BAND = 128


def finish_kernel(y, dwa, first, second, weights, stream, past, block_out, dense_out, total):
    step = pl.program_id(0)
    width = weights.shape[3]

    @pl.when(step == 0)
    def _():
        total[...] = jnp.zeros(total.shape, jnp.float32)

    for row in range(0, total.shape[0], BAND):
        rows = slice(row, row + BAND)
        value = total[rows, :]
        for which, blocks in enumerate((first, second)):
            groups, _, depth = blocks.shape
            matching = weights[which].reshape(groups, depth, width)
            for g in range(groups):
                part = jnp.dot(blocks[g, rows, :], matching[g], preferred_element_type=jnp.float32)
                value += part.astype(jnp.bfloat16).astype(jnp.float32)
        total[rows, :] = value

    @pl.when(step == pl.num_programs(0) - 1)
    def _():
        block = stream[...].astype(jnp.float32) + total[...]
        block_out[...] = block.astype(block_out.dtype)
        dense_out[...] = (dwa[dwa.shape[0] - 1] * block + past[...]).astype(dense_out.dtype)


def finish(y, dwa, blocks, weights, stream, past):
    groups, rows, depth = blocks.shape
    along, across, cut, width = weights.shape
    steps = along // 2
    here = groups // along

    def at(which):
        return lambda i, y: (lax.rem(y[0] + 2 * i + which + along - along // 2, along), 0, 0)

    whole = pl.BlockSpec((rows, width), lambda i, y: (0, 0))
    shape = jax.ShapeDtypeStruct(stream.shape, jnp.bfloat16)
    return pl.pallas_call(
        finish_kernel,
        out_shape=(shape, shape),
        grid_spec=pltpu.PrefetchScalarGridSpec(
            num_scalar_prefetch=1,
            grid=(steps,),
            in_specs=[
                pl.BlockSpec(memory_space=pltpu.SMEM),
                pl.BlockSpec((here, rows, depth), at(0)),
                pl.BlockSpec((here, rows, depth), at(1)),
                pl.BlockSpec((2, across, cut, width), lambda i, y: (i, 0, 0, 0)),
                whole,
                whole,
            ],
            out_specs=(whole, whole),
            scratch_shapes=[pltpu.VMEM(stream.shape, jnp.float32)],
        ),
        name="finish",
    )(y, dwa, blocks, blocks, weights, stream, past)


def columns_here(w_out):
    ctx_count, db_count = lax.axis_size(CTX), lax.axis_size(DB)
    odd = lax.rem(lax.axis_index(CTX), 2)
    half = w_out.shape[0] // 2
    pieces = []
    for flip in range(2):
        route = [
            (c * db_count + d, (2 * d + (c + flip) % 2) * db_count + c // 2)
            for c in range(ctx_count)
            for d in range(db_count)
        ]
        row = (odd + flip) % 2 * half
        send = lax.dynamic_slice_in_dim(w_out, row, half, 0)
        pieces.append(lax.ppermute(send, CTX + DB, route))
    straight = jnp.concatenate(pieces, 1)
    crossed = jnp.concatenate(pieces[::-1], 1)
    return jnp.where(odd == 0, straight, crossed)


def on_device(stream, history, dwa_weights, w_query, w_out, encoded_kv, neighbour_ids):
    tok_rows = stream.shape[0]
    local_heads = w_query.shape[1] // HDIM
    ctx_count = lax.axis_size(CTX)
    db_count = lax.axis_size(DB)
    slots = neighbour_ids.shape[0] // ctx_count
    slab_rows = 2 * encoded_kv.shape[2]
    place = jnp.stack([lax.axis_index("z"), lax.axis_index("core")]).astype(jnp.int32)
    y = lax.axis_index("y").astype(jnp.int32).reshape(1)

    w_in = lax.all_gather(w_query, CTX, axis=0)
    by_head = split_heads(encoded_kv, local_heads)
    store = lax.all_to_all(
        by_head.reshape(db_count, -1, HDIM), DB, split_axis=0, concat_axis=0, tiled=True
    )
    after = shifted(stream[:SPAN], -1)
    own_spans = jnp.concatenate([stream[LEAD:], after[:LEAD]], 0)
    turned = columns_here(w_out)
    turned = lax.all_gather(turned, "x", axis=0)

    picked = pick(neighbour_ids, store.reshape(-1, local_heads * slab_rows, HDIM))
    own_spans, turned, picked = lax.optimization_barrier((own_spans, turned, picked))
    arrived = lax.all_to_all(
        picked.reshape(ctx_count, -1, HDIM), CTX, split_axis=0, concat_axis=0, tiled=True
    ).reshape(ctx_count, slots, local_heads, slab_rows, HDIM)
    mine = around(own_spans, "z")
    past = jnp.sum(history.astype(jnp.float32) * dwa_weights[:-1, None, None], axis=0)
    queries = project(place, mine, partner(mine), w_in)
    spans = tok_rows // SPAN
    last = attend(queries, arrived, spans - 1, 1)
    before = shifted(last, 1)
    rest = attend(queries, arrived, 0, spans - 1)
    attended = jnp.concatenate([before[1:], rest, last[:1]], 0)
    attended, turned = lax.optimization_barrier((attended, turned))
    everyone = lax.all_gather(attended, DB, axis=0)
    columns = around(turned, "y")
    return finish(y, dwa_weights, everyone, columns, stream, past)


def solution(mesh):
    devices = mesh.devices
    cores = 2
    z = devices.shape[1] // cores
    x = 4
    y = devices.shape[0] // x
    split = Mesh(devices.reshape(y, x, z, cores), ("y", "x", "z", "core"))
    placed = (
        P(CTX, DB),
        P(None, CTX, DB),
        P(),
        P(CTX, DB),
        P(DB, CTX),
        P(DB, None, CTX, None, None),
        P(),
    )
    return jax.shard_map(
        on_device,
        mesh=split,
        in_specs=placed,
        out_specs=(P(CTX, DB), P(CTX, DB)),
        check_vma=False,
    )
```

```python
import functools

import jax
import jax.numpy as jnp
from jax import lax
from jax.experimental import pallas as pl
from jax.experimental.pallas import tpu as pltpu
from jax.sharding import Mesh, PartitionSpec as P

ROOM = pltpu.CompilerParams(vmem_limit_bytes=24 * 1024 * 1024)
HDIM = 128
SPAN = 64
NNB = 2
LEAD = SPAN - 1
CTX = ("y", "x")
DB = ("z", "core")


def any_space():
    return pl.BlockSpec(memory_space=pl.ANY)


def vmem_space():
    return pl.BlockSpec(memory_space=pltpu.VMEM)


def split_heads_kernel(source, out, sems):
    heads, local_heads = source.shape[4] // HDIM, out.shape[2]
    copies = []
    for head in range(heads):
        target = out.at[head // local_heads, :, head % local_heads]
        copies.append(
            pltpu.make_async_copy(
                source.at[0, :, :, :, pl.ds(head * HDIM, HDIM)], target, sems.at[head]
            )
        )
        copies[-1].start()
    for copy in copies:
        copy.wait()


def split_heads(encoded, local_heads):
    _, held, rows, pair, width = encoded.shape
    heads = width // HDIM
    return pl.pallas_call(
        split_heads_kernel,
        out_shape=jax.ShapeDtypeStruct(
            (heads // local_heads, held, local_heads, rows, pair, HDIM), encoded.dtype
        ),
        in_specs=[any_space()],
        out_specs=vmem_space(),
        scratch_shapes=[pltpu.SemaphoreType.DMA((heads,))],
        name="split_heads",
    )(encoded)


def pick_kernel(ids, store, out):
    def body(i, carry):
        out[i] = store[ids[i]]
        return carry

    lax.fori_loop(0, out.shape[0], body, 0, unroll=8)


def pick(ids, store):
    count = ids.shape[0]
    block = store.shape[1:]
    return pl.pallas_call(
        pick_kernel,
        out_shape=jax.ShapeDtypeStruct((count,) + block, store.dtype),
        grid_spec=pltpu.PrefetchScalarGridSpec(
            num_scalar_prefetch=1,
            grid=(1,),
            in_specs=[pl.BlockSpec(store.shape, lambda i, s: (0, 0, 0))],
            out_specs=pl.BlockSpec((count,) + block, lambda i, s: (0, 0, 0)),
        ),
        compiler_params=ROOM,
        name="pick",
    )(ids, store)


def attend_kernel(first, q_ref, kv_ref, o_ref):
    slabs, _, heads, rows, _ = kv_ref.shape
    keys = slabs * NNB * rows
    lane = lax.broadcasted_iota(jnp.int32, (SPAN, keys), 1)
    is_key = (lane & 1) == 0
    for at in range(o_ref.shape[0] // SPAN):
        span = first + at
        tokens = slice(span * SPAN, (span + 1) * SPAN)
        for head in range(heads):
            columns = slice(head * HDIM, (head + 1) * HDIM)
            rows_kv = kv_ref[:, NNB * span : NNB * span + NNB, head].reshape(keys, HDIM)
            scores = lax.dot_general(
                q_ref[tokens, columns],
                rows_kv,
                (((1,), (1,)), ((), ())),
                preferred_element_type=jnp.float32,
            ) * HDIM ** (-0.5)
            scores = jnp.where(is_key, scores, -jnp.inf)
            row_max = jnp.max(scores, axis=-1, keepdims=True)
            exponent = jnp.exp(scores - row_max)
            weights = exponent / jnp.sum(exponent, axis=-1, keepdims=True)
            on_values = pltpu.roll(weights, 1, 1).astype(jnp.bfloat16)
            mixed = lax.dot_general(
                on_values, rows_kv, (((1,), (0,)), ((), ())), preferred_element_type=jnp.float32
            )
            o_ref[at * SPAN : (at + 1) * SPAN, columns] = mixed.astype(jnp.bfloat16)


def attend(queries, kv, first, spans):
    return pl.pallas_call(
        functools.partial(attend_kernel, first),
        out_shape=jax.ShapeDtypeStruct((spans * SPAN, queries.shape[1]), jnp.bfloat16),
        in_specs=[vmem_space(), vmem_space()],
        out_specs=vmem_space(),
        compiler_params=ROOM,
    )(queries, kv)


def shifted(block, distance):
    count = lax.axis_size(CTX)
    route = [(i - distance, i) for i in range(count) if 0 <= i - distance < count]
    return lax.ppermute(block, CTX, route)


def ring(count, step):
    return [(i, (i + step) % count) for i in range(count)]


def around(block, axis):
    count = lax.axis_size(axis)
    parts = {0: block}
    right = left = block
    for step in range(1, count // 2 + 1):
        right = lax.ppermute(right, axis, ring(count, 1))
        parts[-step] = right
        if step < count - count // 2:
            left = lax.ppermute(left, axis, ring(count, -1))
            parts[step] = left
    return jnp.stack([parts[i] for i in sorted(parts)])


def partner(block):
    return lax.ppermute(block, "core", [(0, 1), (1, 0)])


def project_kernel(swapped, place, blocks, weights, *rest):
    out = rest[-1]
    steps, rows, depth = blocks.shape
    which = place[1] if not swapped else 1 - place[1]
    for row in range(0, rows, BAND):
        band = slice(row, row + BAND)

        def body(i, total):
            at = lax.rem(place[0] + i + steps - steps // 2, steps) * 2 + which
            matching = weights[pl.ds(at * 2, 2)].reshape(depth, -1)
            return total + jnp.dot(
                blocks[i, band, :], matching, preferred_element_type=jnp.float32
            )

        total = rest[0][band, :] if swapped else jnp.zeros((BAND, out.shape[1]), jnp.float32)
        out[band, :] = lax.fori_loop(0, steps, body, total, unroll=True).astype(out.dtype)


def project(place, blocks, weights, so_far=None):
    rows, width = blocks.shape[1], weights.shape[2]
    swapped = so_far is not None
    terms = (place, blocks, weights) + ((so_far,) if swapped else ())
    return pl.pallas_call(
        functools.partial(project_kernel, swapped),
        out_shape=jax.ShapeDtypeStruct((rows, width), jnp.bfloat16 if swapped else jnp.float32),
        in_specs=[pl.BlockSpec(memory_space=pltpu.SMEM)] + [vmem_space()] * (len(terms) - 1),
        out_specs=vmem_space(),
        compiler_params=ROOM,
        name="project_other" if swapped else "project_own",
    )(*terms)


BAND = 128


def finish_kernel(y, dwa, first, second, weights, stream, past, block_out, dense_out, total):
    step = pl.program_id(0)
    width = weights.shape[3]

    @pl.when(step == 0)
    def _():
        total[...] = jnp.zeros(total.shape, jnp.float32)

    for row in range(0, total.shape[0], BAND):
        rows = slice(row, row + BAND)
        value = total[rows, :]
        for which, blocks in enumerate((first, second)):
            groups, _, depth = blocks.shape
            matching = weights[which].reshape(groups, depth, width)
            for g in range(groups):
                part = jnp.dot(blocks[g, rows, :], matching[g], preferred_element_type=jnp.float32)
                value += part.astype(jnp.bfloat16).astype(jnp.float32)
        total[rows, :] = value

    @pl.when(step == pl.num_programs(0) - 1)
    def _():
        block = stream[...].astype(jnp.float32) + total[...]
        block_out[...] = block.astype(block_out.dtype)
        dense_out[...] = (dwa[dwa.shape[0] - 1] * block + past[...]).astype(dense_out.dtype)


def finish(y, dwa, blocks, weights, stream, past):
    groups, rows, depth = blocks.shape
    along, across, cut, width = weights.shape
    steps = along // 2
    here = groups // along

    def at(which):
        return lambda i, y: (lax.rem(y[0] + 2 * i + which + along - along // 2, along), 0, 0)

    whole = pl.BlockSpec((rows, width), lambda i, y: (0, 0))
    shape = jax.ShapeDtypeStruct(stream.shape, jnp.bfloat16)
    return pl.pallas_call(
        finish_kernel,
        out_shape=(shape, shape),
        grid_spec=pltpu.PrefetchScalarGridSpec(
            num_scalar_prefetch=1,
            grid=(steps,),
            in_specs=[
                pl.BlockSpec(memory_space=pltpu.SMEM),
                pl.BlockSpec((here, rows, depth), at(0)),
                pl.BlockSpec((here, rows, depth), at(1)),
                pl.BlockSpec((2, across, cut, width), lambda i, y: (i, 0, 0, 0)),
                whole,
                whole,
            ],
            out_specs=(whole, whole),
            scratch_shapes=[pltpu.VMEM(stream.shape, jnp.float32)],
        ),
        name="finish",
    )(y, dwa, blocks, blocks, weights, stream, past)


def columns_here(w_out):
    ctx_count, db_count = lax.axis_size(CTX), lax.axis_size(DB)
    odd = lax.rem(lax.axis_index(CTX), 2)
    half = w_out.shape[0] // 2
    pieces = []
    for flip in range(2):
        route = [
            (c * db_count + d, (2 * d + (c + flip) % 2) * db_count + c // 2)
            for c in range(ctx_count)
            for d in range(db_count)
        ]
        row = (odd + flip) % 2 * half
        send = lax.dynamic_slice_in_dim(w_out, row, half, 0)
        pieces.append(lax.ppermute(send, CTX + DB, route))
    straight = jnp.concatenate(pieces, 1)
    crossed = jnp.concatenate(pieces[::-1], 1)
    return jnp.where(odd == 0, straight, crossed)


def on_device(stream, history, dwa_weights, w_query, w_out, encoded_kv, neighbour_ids):
    tok_rows = stream.shape[0]
    local_heads = w_query.shape[1] // HDIM
    ctx_count = lax.axis_size(CTX)
    db_count = lax.axis_size(DB)
    slots = neighbour_ids.shape[0] // ctx_count
    slab_rows = 2 * encoded_kv.shape[2]
    place = jnp.stack([lax.axis_index("z"), lax.axis_index("core")]).astype(jnp.int32)
    y = lax.axis_index("y").astype(jnp.int32).reshape(1)

    w_in = lax.all_gather(w_query, CTX, axis=0)
    by_head = split_heads(encoded_kv, local_heads)
    store = lax.all_to_all(
        by_head.reshape(db_count, -1, HDIM), DB, split_axis=0, concat_axis=0, tiled=True
    )
    after = shifted(stream[:SPAN], -1)
    own_spans = jnp.concatenate([stream[LEAD:], after[:LEAD]], 0)
    turned = columns_here(w_out)
    turned = lax.all_gather(turned, "x", axis=0)

    picked = pick(neighbour_ids, store.reshape(-1, local_heads * slab_rows, HDIM))
    turned, picked = lax.optimization_barrier((turned, picked))
    arrived = lax.all_to_all(
        picked.reshape(ctx_count, -1, HDIM), CTX, split_axis=0, concat_axis=0, tiled=True
    ).reshape(ctx_count, slots, local_heads, slab_rows, HDIM)
    mine = around(own_spans, "z")
    past = jnp.sum(history.astype(jnp.float32) * dwa_weights[:-1, None, None], axis=0)
    other = partner(mine)
    queries = project(place, mine, w_in)
    queries = project(place, other, w_in, queries)
    spans = tok_rows // SPAN
    last = attend(queries, arrived, spans - 1, 1)
    before = shifted(last, 1)
    rest = attend(queries, arrived, 0, spans - 1)
    attended = jnp.concatenate([before[1:], rest, last[:1]], 0)
    everyone = lax.all_gather(attended, DB, axis=0)
    columns = around(turned, "y")
    return finish(y, dwa_weights, everyone, columns, stream, past)


def solution(mesh):
    devices = mesh.devices
    cores = 2
    z = devices.shape[1] // cores
    x = 4
    y = devices.shape[0] // x
    split = Mesh(devices.reshape(y, x, z, cores), ("y", "x", "z", "core"))
    placed = (
        P(CTX, DB),
        P(None, CTX, DB),
        P(),
        P(CTX, DB),
        P(DB, CTX),
        P(DB, None, CTX, None, None),
        P(),
    )
    return jax.shard_map(
        on_device,
        mesh=split,
        in_specs=placed,
        out_specs=(P(CTX, DB), P(CTX, DB)),
        check_vma=False,
    )
```

```python
import functools

import jax
import jax.numpy as jnp
from jax import lax
from jax.experimental import pallas as pl
from jax.experimental.pallas import tpu as pltpu
from jax.sharding import Mesh, PartitionSpec as P

ROOM = pltpu.CompilerParams(vmem_limit_bytes=24 * 1024 * 1024)
HDIM = 128
SPAN = 64
NNB = 2
LEAD = SPAN - 1
CTX = ("y", "x")
DB = ("z", "core")


def any_space():
    return pl.BlockSpec(memory_space=pl.ANY)


def vmem_space():
    return pl.BlockSpec(memory_space=pltpu.VMEM)


def split_heads_kernel(source, out, sems):
    heads, local_heads = source.shape[4] // HDIM, out.shape[2]
    copies = []
    for head in range(heads):
        target = out.at[head // local_heads, :, head % local_heads]
        copies.append(
            pltpu.make_async_copy(
                source.at[0, :, :, :, pl.ds(head * HDIM, HDIM)], target, sems.at[head]
            )
        )
        copies[-1].start()
    for copy in copies:
        copy.wait()


def split_heads(encoded, local_heads):
    _, held, rows, pair, width = encoded.shape
    heads = width // HDIM
    return pl.pallas_call(
        split_heads_kernel,
        out_shape=jax.ShapeDtypeStruct(
            (heads // local_heads, held, local_heads, rows, pair, HDIM), encoded.dtype
        ),
        in_specs=[any_space()],
        out_specs=vmem_space(),
        scratch_shapes=[pltpu.SemaphoreType.DMA((heads,))],
        name="split_heads",
    )(encoded)


def pick_kernel(ids, store, out, picked, sems):
    parts = sems.shape[0]
    count = out.shape[0] // parts

    def body(i, carry):
        picked[i] = store[ids[i]]
        return carry

    copies = []
    for part in range(parts):
        here = pl.ds(part * count, count)
        lax.fori_loop(part * count, (part + 1) * count, body, 0, unroll=16)
        copies.append(pltpu.make_async_copy(picked.at[here], out.at[here], sems.at[part]))
        copies[-1].start()
    for copy in copies:
        copy.wait()


def pick(ids, store):
    shape = (ids.shape[0],) + store.shape[1:]
    return pl.pallas_call(
        pick_kernel,
        out_shape=jax.ShapeDtypeStruct(shape, store.dtype),
        in_specs=[pl.BlockSpec(memory_space=pltpu.SMEM), vmem_space()],
        out_specs=pl.BlockSpec(memory_space=pltpu.HBM),
        scratch_shapes=[pltpu.VMEM(shape, store.dtype), pltpu.SemaphoreType.DMA((4,))],
        compiler_params=ROOM,
        name="pick",
    )(ids, store)


def attend_kernel(first, q_ref, kv_ref, o_ref):
    slabs, _, heads, rows, _ = kv_ref.shape
    keys = slabs * NNB * rows
    lane = lax.broadcasted_iota(jnp.int32, (SPAN, keys), 1)
    is_key = (lane & 1) == 0
    for at in range(o_ref.shape[0] // SPAN):
        span = first + at
        tokens = slice(span * SPAN, (span + 1) * SPAN)
        for head in range(heads):
            columns = slice(head * HDIM, (head + 1) * HDIM)
            rows_kv = kv_ref[:, NNB * span : NNB * span + NNB, head].reshape(keys, HDIM)
            scores = lax.dot_general(
                q_ref[tokens, columns],
                rows_kv,
                (((1,), (1,)), ((), ())),
                preferred_element_type=jnp.float32,
            ) * HDIM ** (-0.5)
            scores = jnp.where(is_key, scores, -jnp.inf)
            row_max = jnp.max(scores, axis=-1, keepdims=True)
            exponent = jnp.exp(scores - row_max)
            weights = exponent / jnp.sum(exponent, axis=-1, keepdims=True)
            on_values = pltpu.roll(weights, 1, 1).astype(jnp.bfloat16)
            mixed = lax.dot_general(
                on_values, rows_kv, (((1,), (0,)), ((), ())), preferred_element_type=jnp.float32
            )
            o_ref[at * SPAN : (at + 1) * SPAN, columns] = mixed.astype(jnp.bfloat16)


def attend(queries, kv, first, spans):
    return pl.pallas_call(
        functools.partial(attend_kernel, first),
        out_shape=jax.ShapeDtypeStruct((spans * SPAN, queries.shape[1]), jnp.bfloat16),
        in_specs=[vmem_space(), vmem_space()],
        out_specs=vmem_space(),
        compiler_params=ROOM,
    )(queries, kv)


def shifted(block, distance):
    count = lax.axis_size(CTX)
    route = [(i - distance, i) for i in range(count) if 0 <= i - distance < count]
    return lax.ppermute(block, CTX, route)


def ring(count, step):
    return [(i, (i + step) % count) for i in range(count)]


def around(block, axis):
    count = lax.axis_size(axis)
    parts = {0: block}
    right = left = block
    for step in range(1, count // 2 + 1):
        right = lax.ppermute(right, axis, ring(count, 1))
        parts[-step] = right
        if step < count - count // 2:
            left = lax.ppermute(left, axis, ring(count, -1))
            parts[step] = left
    return jnp.stack([parts[i] for i in sorted(parts)])


def partner(block):
    return lax.ppermute(block, "core", [(0, 1), (1, 0)])


def project_kernel(swapped, place, blocks, weights, *rest):
    out = rest[-1]
    steps, rows, depth = blocks.shape
    which = place[1] if not swapped else 1 - place[1]
    for row in range(0, rows, BAND):
        band = slice(row, row + BAND)

        def body(i, total):
            at = lax.rem(place[0] + i + steps - steps // 2, steps) * 2 + which
            matching = weights[pl.ds(at * 2, 2)].reshape(depth, -1)
            return total + jnp.dot(
                blocks[i, band, :], matching, preferred_element_type=jnp.float32
            )

        total = rest[0][band, :] if swapped else jnp.zeros((BAND, out.shape[1]), jnp.float32)
        out[band, :] = lax.fori_loop(0, steps, body, total, unroll=True).astype(out.dtype)


def project(place, blocks, weights, so_far=None):
    rows, width = blocks.shape[1], weights.shape[2]
    swapped = so_far is not None
    terms = (place, blocks, weights) + ((so_far,) if swapped else ())
    return pl.pallas_call(
        functools.partial(project_kernel, swapped),
        out_shape=jax.ShapeDtypeStruct((rows, width), jnp.bfloat16 if swapped else jnp.float32),
        in_specs=[pl.BlockSpec(memory_space=pltpu.SMEM)] + [vmem_space()] * (len(terms) - 1),
        out_specs=vmem_space(),
        compiler_params=ROOM,
        name="project_other" if swapped else "project_own",
    )(*terms)


BAND = 128


def finish_kernel(y, dwa, gathered, weights, stream, past, block_out, dense_out, blocks, sems):
    along, _, _, width = weights.shape
    here = gathered.shape[0] // along
    depth = gathered.shape[2]
    copies = []
    for k in range(along):
        source = lax.rem(y[0] + k + along - along // 2, along) * here
        copies.append(
            pltpu.make_async_copy(
                gathered.at[pl.ds(source, here)], blocks.at[pl.ds(k * here, here)], sems.at[k]
            )
        )
        copies[-1].start()
    for row in range(0, stream.shape[0], BAND):
        rows = slice(row, row + BAND)
        total = jnp.zeros((BAND, width), jnp.float32)
        for k in range(along):
            if row == 0:
                copies[k].wait()
            matching = weights[k].reshape(here, depth, width)
            for g in range(here):
                part = jnp.dot(
                    blocks[k * here + g, rows, :], matching[g], preferred_element_type=jnp.float32
                )
                total += part.astype(jnp.bfloat16).astype(jnp.float32)
        block = stream[rows, :].astype(jnp.float32) + total
        block_out[rows, :] = block.astype(block_out.dtype)
        dense_out[rows, :] = (dwa[dwa.shape[0] - 1] * block + past[rows, :]).astype(dense_out.dtype)


def finish(y, dwa, gathered, columns, stream, past):
    shape = jax.ShapeDtypeStruct(stream.shape, jnp.bfloat16)
    scalars = pl.BlockSpec(memory_space=pltpu.SMEM)
    return pl.pallas_call(
        finish_kernel,
        out_shape=(shape, shape),
        in_specs=[scalars] * 2 + [pl.BlockSpec(memory_space=pltpu.HBM)] + [vmem_space()] * 3,
        out_specs=(vmem_space(), vmem_space()),
        scratch_shapes=[
            pltpu.VMEM(gathered.shape, gathered.dtype),
            pltpu.SemaphoreType.DMA((columns.shape[0],)),
        ],
        compiler_params=pltpu.CompilerParams(vmem_limit_bytes=50 * 1024 * 1024),
        name="finish",
    )(y, dwa, gathered, columns, stream, past)


def columns_here(w_out):
    ctx_count, db_count = lax.axis_size(CTX), lax.axis_size(DB)
    odd = lax.rem(lax.axis_index(CTX), 2)
    half = w_out.shape[0] // 2
    pieces = []
    for flip in range(2):
        route = [
            (c * db_count + d, (2 * d + (c + flip) % 2) * db_count + c // 2)
            for c in range(ctx_count)
            for d in range(db_count)
        ]
        row = (odd + flip) % 2 * half
        send = lax.dynamic_slice_in_dim(w_out, row, half, 0)
        pieces.append(lax.ppermute(send, CTX + DB, route))
    straight = jnp.concatenate(pieces, 1)
    crossed = jnp.concatenate(pieces[::-1], 1)
    return jnp.where(odd == 0, straight, crossed)


def on_device(stream, history, dwa_weights, w_query, w_out, encoded_kv, neighbour_ids):
    tok_rows = stream.shape[0]
    local_heads = w_query.shape[1] // HDIM
    ctx_count = lax.axis_size(CTX)
    db_count = lax.axis_size(DB)
    slots = neighbour_ids.shape[0] // ctx_count
    slab_rows = 2 * encoded_kv.shape[2]
    place = jnp.stack([lax.axis_index("z"), lax.axis_index("core")]).astype(jnp.int32)
    y = lax.axis_index("y").astype(jnp.int32).reshape(1)

    w_in = lax.all_gather(w_query, CTX, axis=0)
    by_head = split_heads(encoded_kv, local_heads)
    store = lax.all_to_all(
        by_head.reshape(db_count, -1, HDIM), DB, split_axis=0, concat_axis=0, tiled=True
    )
    after = shifted(stream[:SPAN], -1)
    own_spans = jnp.concatenate([stream[LEAD:], after[:LEAD]], 0)
    turned = columns_here(w_out)
    turned = lax.all_gather(turned, "x", axis=0)

    picked = pick(neighbour_ids, store.reshape(-1, local_heads * slab_rows, HDIM))
    turned, picked = lax.optimization_barrier((turned, picked))
    arrived = lax.all_to_all(
        picked.reshape(ctx_count, -1, HDIM), CTX, split_axis=0, concat_axis=0, tiled=True
    ).reshape(ctx_count, slots, local_heads, slab_rows, HDIM)
    mine = around(own_spans, "z")
    past = jnp.sum(history.astype(jnp.float32) * dwa_weights[:-1, None, None], axis=0)
    other = partner(mine)
    queries = project(place, mine, w_in)
    queries = project(place, other, w_in, queries)
    spans = tok_rows // SPAN
    last = attend(queries, arrived, spans - 1, 1)
    before = shifted(last, 1)
    rest = attend(queries, arrived, 0, spans - 1)
    attended = jnp.concatenate([before[1:], rest, last[:1]], 0)
    everyone = lax.all_gather(attended, DB, axis=0)
    columns = around(turned, "y")
    return finish(y, dwa_weights, everyone, columns, stream, past)


def solution(mesh):
    devices = mesh.devices
    cores = 2
    z = devices.shape[1] // cores
    x = 4
    y = devices.shape[0] // x
    split = Mesh(devices.reshape(y, x, z, cores), ("y", "x", "z", "core"))
    placed = (
        P(CTX, DB),
        P(None, CTX, DB),
        P(),
        P(CTX, DB),
        P(DB, CTX),
        P(DB, None, CTX, None, None),
        P(),
    )
    return jax.shard_map(
        on_device,
        mesh=split,
        in_specs=placed,
        out_specs=(P(CTX, DB), P(CTX, DB)),
        check_vma=False,
    )
```
